32 devices in a mesh: cable: 16 (over z, y, x), win: 2 (over core).
Axes of the slice: x: 2, y: 2, z: 4, core: 2. Of those that a mesh axis runs over, the one named last changes fastest.
Arguments:
- records: bfloat16 [512, 512, 128], P(None, 'cable', 'win'), may hold values from -60 to 60
Outputs:
- xcorr: float32 [512, 64, 512], P('cable', None, 'win')
The draws below stay inside these ranges and needn't reach their ends.
All inputs are finite; a program needn't handle non-finite values.
Results may differ from the reference program's by a relative error of at most 0.0064.
Values may be sent and summed in bfloat16 or wider, within the bound.
No kernel may reach another device: no remote copies, remote signals or barrier semaphores. Data moves between devices by JAX's collectives and lax.ppermute only.
A program may use at most 128 MiB of HBM per device.

```python
import math
import jax
import jax.numpy as jnp
from jax import lax

SAMPLES = 512
OFFS = 64
CHANNELS = 512
WINDOWS = 128


def draw_records(key, part):
    keys = jax.random.split(jax.random.fold_in(key, 17), 3)
    base = jax.random.normal(keys[0], (SAMPLES, CHANNELS, WINDOWS), jnp.float32)
    colour = jax.random.uniform(keys[1], (1, CHANNELS, 1), jnp.float32, -0.8, 0.8)
    mixed = base + colour * jnp.roll(base, 1, axis=0)
    scale = jnp.exp(jax.random.uniform(keys[2], (1, CHANNELS, WINDOWS), jnp.float32, 0.0, math.log(10.0)))
    return jnp.clip(mixed * scale, -60.0, 60.0).astype(jnp.bfloat16)


def setup_inputs(seed: int = 0) -> dict:
    streams_of = jax.random.split(jax.random.key(seed), 2)
    records = draw_records(jax.random.fold_in(streams_of[1], 71), 0)
    return {"records": records}


epsilon = 1e-06

def forward_table(samples):
    frequencies = samples // 2 + 1
    times = jnp.arange(samples, dtype=jnp.int32)[None, :]
    freq = jnp.arange(frequencies, dtype=jnp.int32)[:, None]
    phase = 2.0 * math.pi / samples * (freq * times % samples).astype(jnp.float32)
    taper = 0.5 - 0.5 * jnp.cos(2.0 * math.pi / samples * times.astype(jnp.float32))
    return jnp.concatenate([taper * jnp.cos(phase), -taper * jnp.sin(phase)], axis=0).astype(jnp.bfloat16)

def inverse_table(samples, lag_start, lag_count, factor):
    frequencies = samples // 2 + 1
    freq = jnp.arange(frequencies, dtype=jnp.int32)[:, None]
    lagpos = lag_start + jnp.arange(lag_count, dtype=jnp.int32)[None, :]
    phase = 2.0 * math.pi / samples * (freq * lagpos % samples).astype(jnp.float32)
    weight = jnp.where((freq == 0) | (freq == samples // 2), 1.0, 2.0).astype(jnp.float32) * factor
    return jnp.concatenate([weight * jnp.cos(phase), -weight * jnp.sin(phase)], axis=0)

def reference(records):
    samples, channels, windows = records.shape
    frequencies = samples // 2 + 1
    table = forward_table(samples)
    spectra = jnp.dot(table, records.reshape(samples, channels * windows), preferred_element_type=jnp.float32)
    spectra = spectra.reshape(2 * frequencies, channels, windows)
    real_part = spectra[:frequencies]
    imag_part = spectra[frequencies:]
    power = lax.optimization_barrier(jnp.sum(real_part * real_part + imag_part * imag_part, axis=2)) / windows
    scaling = lax.rsqrt(power + epsilon)[:, :, None]
    packed = jnp.concatenate([real_part * scaling, imag_part * scaling], axis=2).astype(jnp.bfloat16)
    flipped = jnp.concatenate([packed[:, :, windows:], -packed[:, :, :windows]], axis=2)
    padded = jnp.pad(packed, ((0, 0), (0, OFFS), (0, 0)))
    lefthand = packed.astype(jnp.float32)
    flipped_wide = flipped.astype(jnp.float32)

    def one_offset(offset):
        partner = lax.dynamic_slice_in_dim(padded, (offset + 1).astype(jnp.int32), channels, 1).astype(jnp.float32)
        real_sum = lax.optimization_barrier(jnp.sum(lefthand * partner, axis=2))
        imag_sum = lax.optimization_barrier(jnp.sum(flipped_wide * partner, axis=2))
        return jnp.concatenate([real_sum, imag_sum], axis=0)
    cross = lax.map(one_offset, jnp.arange(OFFS, dtype=jnp.int32))
    factor = 1.0 / math.sqrt(2.0 * windows * frequencies)
    inverse = inverse_table(samples, 0, samples, factor)
    return jnp.einsum('kxc,xl->ckl', cross, inverse, precision=lax.Precision.HIGHEST)
```

```python
import functools
import math

import jax
import jax.numpy as jnp
from jax import lax
from jax.experimental import pallas as pl
from jax.experimental.pallas import tpu as pltpu
from jax.sharding import PartitionSpec as P

OFFS = 64
GROUP = 4
CHUNKS = (11, 11, 11)

epsilon = 1e-06

VMEM = pl.BlockSpec(memory_space=pltpu.VMEM)
SMEM = pl.BlockSpec(memory_space=pltpu.SMEM)
NT = (((1,), (1,)), ((), ()))
TN = (((0,), (0,)), ((), ()))


def odd_pitch(rows):
    return rows + 1 - rows % 2


def forward_kernel(sizes, windows_total, table_ref, own_ref, other_ref, *refs):
    outs, scratch = refs[:-1], refs[-1]
    channels, windows, samples = own_ref.shape
    rows = table_ref.shape[0]
    pitch = odd_pitch(rows)

    def transform(p, carry):
        both = jnp.concatenate(
            [own_ref[2 * p], other_ref[2 * p], own_ref[2 * p + 1], other_ref[2 * p + 1]], axis=0
        )
        spec = lax.dot_general(table_ref[...], both, NT, preferred_element_type=jnp.float32)
        width = 2 * windows
        scratch[pl.ds(2 * p * pitch, rows), :] = spec[:, :width]
        scratch[pl.ds((2 * p + 1) * pitch, rows), :] = spec[:, width:]
        return carry

    for p in range(channels // 2):
        transform(p, 0)

    row = 0
    for size, out in zip(sizes, outs):

        def whiten(f, carry, row=row, size=size, out=out):
            re = scratch[pl.ds(row + f, channels, stride=pitch), :]
            im = scratch[pl.ds(row + size + f, channels, stride=pitch), :]
            power = jnp.sum(re * re + im * im, axis=1, keepdims=True) / windows_total
            scale = lax.rsqrt(power + epsilon)
            out[f, :, : 2 * windows] = (re * scale).astype(jnp.bfloat16)
            out[f, :, 2 * windows :] = (im * scale).astype(jnp.bfloat16)
            return carry

        lax.fori_loop(0, size, whiten, 0, unroll=True)
        row += 2 * size


def forward(table, sizes, own, other, windows_total):
    channels, windows, samples = own.shape
    rows = table.shape[0]
    return pl.pallas_call(
        functools.partial(forward_kernel, sizes, windows_total),
        out_shape=[
            jax.ShapeDtypeStruct((s, channels, 4 * windows), jnp.bfloat16) for s in sizes
        ],
        in_specs=[VMEM] * 3,
        out_specs=[VMEM] * len(sizes),
        scratch_shapes=[pltpu.VMEM((channels * odd_pitch(rows), 2 * windows), jnp.float32)],
        cost_estimate=pl.CostEstimate(
            flops=2 * rows * samples * channels * windows * 2,
            bytes_accessed=4 * channels * windows * samples + 2 * rows * channels * windows * 2,
            transcendentals=0,
        ),
        name="forward",
    )(table, own, other)


def cross_kernel(place_ref, *refs):
    group = GROUP
    own, halo_ref = refs[:group], refs[group]
    outs, rows_ref = refs[group + 1 : -1], refs[-1]
    size, channels, width = own[0].shape
    halo = halo_ref.shape[0]
    half = width // 2
    place = place_ref[0]
    for m in range(group):
        start = pl.multiple_of((place ^ m) * channels, channels)
        rows_ref[:, pl.ds(start, channels), :] = own[m][...]
    for h in range(halo):
        rows_ref[:, pl.ds((group + h) * channels, channels), :] = halo_ref[h]
    breadth = 128
    pairs = channels // 2
    lane = lax.broadcasted_iota(jnp.int32, (pairs, breadth), 1)
    low = lane < OFFS
    row = lax.broadcasted_iota(jnp.int32, (channels, breadth), 0)
    masks = [(row >> bit) % 2 == 1 for bit in range(3)]

    def one(f, carry):
        for m in range(group):
            start = pl.multiple_of((place ^ m) * channels, channels)
            left = own[m][f]
            a, b = left[:, :half], left[:, half:]
            lefthand = jnp.concatenate(
                [jnp.concatenate([a, b], axis=1), jnp.concatenate([b, -a], axis=1)], axis=0
            )
            partner = rows_ref[f, pl.ds(start, breadth), :]
            prod = lax.dot_general(lefthand, partner, NT, preferred_element_type=jnp.float32)
            pieces = []
            for part in range(2):
                sides = []
                for side in range(2):
                    first = (2 * part + side) * pairs
                    slabs = []
                    for r in range(0, pairs, 8):
                        slab = prod[first + r : first + r + 8]
                        shift = (breadth - 1 - side * (pairs - OFFS) - r) % breadth
                        slabs.append(pltpu.roll(slab, shift, 1))
                    sides.append(jnp.concatenate(slabs, axis=0))
                both = jnp.concatenate(sides, axis=0)
                for bit, mask in enumerate(masks):
                    both = jnp.where(mask, pltpu.roll(both, breadth - (1 << bit), 1), both)
                pieces.append(jnp.where(low, both[:pairs], both[pairs:]))
            outs[m][f] = jnp.concatenate(pieces, axis=0).astype(jnp.bfloat16)
        return carry

    lax.fori_loop(0, size, one, 0, unroll=True)


def correlate(place, own, halo):
    size, channels, width = own[0].shape
    rows = (GROUP + halo.shape[0] + 1) * channels
    return pl.pallas_call(
        cross_kernel,
        out_shape=[jax.ShapeDtypeStruct((size, channels, 2 * OFFS), jnp.bfloat16)] * GROUP,
        in_specs=[SMEM] + [VMEM] * (GROUP + 1),
        out_specs=[VMEM] * GROUP,
        scratch_shapes=[pltpu.VMEM((size, rows, width), jnp.bfloat16)],
        cost_estimate=pl.CostEstimate(
            flops=2 * size * GROUP * 2 * channels * 128 * width,
            bytes_accessed=2 * size * channels * width * (GROUP + 2),
            transcendentals=0,
        ),
        name="correlate",
    )(place, *own, halo)


def inverse_kernel(sets, cos_ref, sin_ref, *refs):
    parts, out_ref, scratch = refs[:sets], refs[sets], refs[sets + 1]
    rows = cos_ref.shape[0]
    pitch = odd_pitch(rows)
    base = 0
    for part in parts:
        count, channels, width = part.shape

        def spread(x, carry, part=part, base=base, channels=channels):
            scratch[pl.ds(base + x, channels, stride=pitch), :] = part[x].astype(jnp.float32)
            return carry

        lax.fori_loop(0, count, spread, 0, unroll=True)
        base += count
    pairs = channels // 2
    for p in range(pairs):
        re = scratch[pl.ds(p * pitch, rows), :].astype(jnp.bfloat16)
        im = scratch[pl.ds((pairs + p) * pitch, rows), :].astype(jnp.bfloat16)
        result = lax.dot_general(re, cos_ref[...], TN, preferred_element_type=jnp.float32)
        result += lax.dot_general(im, sin_ref[...], TN, preferred_element_type=jnp.float32)
        out_ref[p] = result[:OFFS]
        out_ref[pairs + p] = result[OFFS:]


def inverse(cosines, sines, parts):
    rows, lags = cosines.shape
    channels = parts[0].shape[1]
    return pl.pallas_call(
        functools.partial(inverse_kernel, len(parts)),
        out_shape=jax.ShapeDtypeStruct((channels, OFFS, lags), jnp.float32),
        in_specs=[VMEM] * (2 + len(parts)),
        out_specs=VMEM,
        scratch_shapes=[pltpu.VMEM((channels * odd_pitch(rows), 2 * OFFS), jnp.float32)],
        cost_estimate=pl.CostEstimate(
            flops=4 * rows * channels * OFFS * lags,
            bytes_accessed=4 * channels * OFFS * lags + 4 * rows * channels * OFFS,
            transcendentals=0,
        ),
        name="inverse",
    )(cosines, sines, *parts)


def phases(freq, pos, samples):
    return 2.0 * math.pi / samples * (freq * pos % samples).astype(jnp.float32)


def forward_table(freq, samples):
    times = jnp.arange(samples, dtype=jnp.int32)
    phase = phases(freq[:, :, None], times, samples)
    taper = 0.5 - 0.5 * jnp.cos(2.0 * math.pi / samples * times.astype(jnp.float32))
    both = jnp.stack([taper * jnp.cos(phase), -taper * jnp.sin(phase)], axis=1)
    return both.reshape(-1, samples).astype(jnp.bfloat16)


def inverse_tables(freq, samples, lag_start, lag_count, factor):
    lagpos = lag_start + jnp.arange(lag_count, dtype=jnp.int32)[None, :]
    freq = freq[:, None]
    phase = phases(freq, lagpos, samples)
    weight = jnp.where((freq == 0) | (freq == samples // 2), 1.0, 2.0)
    weight = jnp.where(freq > samples // 2, 0.0, weight).astype(jnp.float32) * factor
    return (
        (weight * jnp.cos(phase)).astype(jnp.bfloat16),
        (-weight * jnp.sin(phase)).astype(jnp.bfloat16),
    )


def body(records):
    samples, channels, windows = records.shape
    frequencies = samples // 2 + 1
    halves = lax.axis_size("win")
    blocks = lax.axis_size("cable")
    total_windows = windows * halves
    group = GROUP
    members = group * halves
    halo = -(-OFFS // channels)
    chunks = CHUNKS
    starts = [sum(chunks[:q]) for q in range(len(chunks))]
    assert sum(chunks) * members >= frequencies and blocks % group == 0 and halves == 2
    assert halo < group and channels + OFFS <= 128
    me = lax.axis_index("cable")
    place = lax.rem(me, group)
    half = lax.axis_index("win")

    def exchange(block, m):
        if m == 0:
            return block
        return lax.ppermute(block, "cable", [(i, i ^ m) for i in range(blocks)])

    def sibling(block):
        return lax.ppermute(block, "win", [(i, 1 - i) for i in range(halves)])

    own = jnp.transpose(records, (1, 2, 0))
    other = sibling(own)

    def freqs(q, m, side):
        row = starts[q] + jnp.arange(chunks[q], dtype=jnp.int32)
        return row * members + (place ^ m) * halves + side

    tables = [
        forward_table(jnp.stack([freqs(q, m, half) for m in range(group)]), samples)
        for q in range(len(chunks))
    ]
    table = jnp.concatenate(tables, axis=0)
    sizes = [size for size in chunks for _ in range(group)]
    white = forward(table, sizes, own, other, total_windows)

    place_arr = place.reshape(1).astype(jnp.int32)
    shares = [
        [exchange(white[q * group + m], m) for m in range(group)] for q in range(len(chunks))
    ]
    crosses = []
    for q in range(len(chunks)):
        share = shares[q]
        edge = []
        for h in range(halo):
            block = share[0]
            for m in range(1, group):
                block = jnp.where((place ^ m) == h, share[m], block)
            edge.append(block)
        edge = lax.ppermute(
            jnp.stack(edge), "cable", [(i, i - group) for i in range(group, blocks)]
        )
        crosses.append(correlate(place_arr, share, edge))
    parts = []
    for q in range(len(chunks)):
        mine = jnp.concatenate([exchange(crosses[q][m], m) for m in range(group)], axis=0)
        parts += [mine, sibling(mine)]
    freq = jnp.concatenate(
        [
            freqs(q, m, side)
            for q in range(len(chunks))
            for side in (half, 1 - half)
            for m in range(group)
        ]
    )
    lag_count = samples // halves
    factor = 1.0 / math.sqrt(2.0 * total_windows * frequencies)
    cosines, sines = inverse_tables(freq, samples, half * lag_count, lag_count, factor)
    return inverse(cosines, sines, parts)


def solution(mesh):
    return jax.shard_map(
        body,
        mesh=mesh,
        in_specs=(P(None, "cable", "win"),),
        out_specs=P("cable", None, "win"),
        check_vma=False,
    )
```

```python
import functools
import math

import jax
import jax.numpy as jnp
from jax import lax
from jax.experimental import pallas as pl
from jax.experimental.pallas import tpu as pltpu
from jax.sharding import PartitionSpec as P

OFFS = 64
GROUP = 4
ORDER = (3, 1, 2)
CHUNKS = (12, 12, 9)

epsilon = 1e-06

VMEM = pl.BlockSpec(memory_space=pltpu.VMEM)
SMEM = pl.BlockSpec(memory_space=pltpu.SMEM)
NT = (((1,), (1,)), ((), ()))
TN = (((0,), (0,)), ((), ()))


def odd_pitch(rows):
    return rows + 1 - rows % 2


def forward_kernel(sizes, windows_total, table_ref, own_ref, other_ref, *refs):
    outs, scratch = refs[:-1], refs[-1]
    channels, windows, _ = own_ref.shape
    rows = table_ref.shape[0]
    pitch = odd_pitch(rows)

    def transform(p, carry):
        both = jnp.concatenate(
            [own_ref[2 * p], other_ref[2 * p], own_ref[2 * p + 1], other_ref[2 * p + 1]], axis=0
        )
        spec = lax.dot_general(table_ref[...], both, NT, preferred_element_type=jnp.float32)
        width = 2 * windows
        scratch[pl.ds(2 * p * pitch, rows), :] = spec[:, :width]
        scratch[pl.ds((2 * p + 1) * pitch, rows), :] = spec[:, width:]
        return carry

    for p in range(channels // 2):
        transform(p, 0)

    row = 0
    for size, out in zip(sizes, outs):

        def whiten(f, carry, row=row, size=size, out=out):
            re = scratch[pl.ds(row + f, channels, stride=pitch), :]
            im = scratch[pl.ds(row + size + f, channels, stride=pitch), :]
            power = jnp.sum(re * re + im * im, axis=1, keepdims=True) / windows_total
            scale = lax.rsqrt(power + epsilon)
            out[f, :, : 2 * windows] = (re * scale).astype(jnp.bfloat16)
            out[f, :, 2 * windows :] = (im * scale).astype(jnp.bfloat16)
            return carry

        lax.fori_loop(0, size, whiten, 0, unroll=True)
        row += 2 * size


def forward(table, sizes, own, other, windows_total):
    channels, windows, samples = own.shape
    rows = table.shape[0]
    return pl.pallas_call(
        functools.partial(forward_kernel, sizes, windows_total),
        out_shape=[
            jax.ShapeDtypeStruct((s, channels, 4 * windows), jnp.bfloat16) for s in sizes
        ],
        in_specs=[VMEM] * 3,
        out_specs=[VMEM] * len(sizes),
        scratch_shapes=[pltpu.VMEM((channels * odd_pitch(rows), 2 * windows), jnp.float32)],
        cost_estimate=pl.CostEstimate(
            flops=2 * rows * samples * channels * windows * 2,
            bytes_accessed=4 * channels * windows * samples + 2 * rows * channels * windows * 2,
            transcendentals=0,
        ),
        compiler_params=pltpu.CompilerParams(vmem_limit_bytes=8 << 20),
        name="forward",
    )(table, own, other)


def edge_kernel(place_ref, *refs):
    shares, out_ref = refs[:GROUP], refs[-1]
    for m in range(GROUP):
        block = place_ref[0] ^ m

        @pl.when(block < out_ref.shape[0])
        def _(m=m, block=block):
            out_ref[block] = shares[m][...]


def edge(place, shares, halo, after):
    shape = (halo,) + shares[0].shape
    return pl.pallas_call(
        edge_kernel,
        out_shape=jax.ShapeDtypeStruct(shape, jnp.bfloat16),
        in_specs=[SMEM] + [VMEM] * GROUP + [pl.BlockSpec(memory_space=pl.ANY)] * len(after),
        out_specs=VMEM,
        compiler_params=pltpu.CompilerParams(vmem_limit_bytes=4 << 20),
        name="edge",
    )(place, *shares, *after)


def cross_kernel(place_ref, *refs):
    group = GROUP
    own, halo_ref = refs[:group], refs[group]
    outs, rows_ref = refs[group + 1 : -1], refs[-1]
    size, channels, width = own[0].shape
    halo = halo_ref.shape[0]
    half = width // 2
    place = place_ref[0]
    for m in range(group):
        start = pl.multiple_of((place ^ m) * channels, channels)
        rows_ref[:, pl.ds(start, channels), :] = own[m][...]
    for h in range(halo):
        rows_ref[:, pl.ds((group + h) * channels, channels), :] = halo_ref[h]
    breadth = 128
    pairs = channels // 2
    lane = lax.broadcasted_iota(jnp.int32, (pairs, breadth), 1)
    low = lane < OFFS
    row = lax.broadcasted_iota(jnp.int32, (channels, breadth), 0)
    masks = [(row >> bit) % 2 == 1 for bit in range(3)]

    def one(f, carry):
        for m in range(group):
            start = pl.multiple_of((place ^ m) * channels, channels)
            left = own[m][f]
            a, b = left[:, :half], left[:, half:]
            lefthand = jnp.concatenate(
                [jnp.concatenate([a, b], axis=1), jnp.concatenate([b, -a], axis=1)], axis=0
            )
            partner = rows_ref[f, pl.ds(start, breadth), :]
            prod = lax.dot_general(lefthand, partner, NT, preferred_element_type=jnp.float32)
            pieces = []
            for part in range(2):
                sides = []
                for side in range(2):
                    first = (2 * part + side) * pairs
                    slabs = []
                    for r in range(0, pairs, 8):
                        slab = prod[first + r : first + r + 8]
                        shift = (breadth - 1 - side * (pairs - OFFS) - r) % breadth
                        slabs.append(pltpu.roll(slab, shift, 1))
                    sides.append(jnp.concatenate(slabs, axis=0))
                both = jnp.concatenate(sides, axis=0)
                for bit, mask in enumerate(masks):
                    both = jnp.where(mask, pltpu.roll(both, breadth - (1 << bit), 1), both)
                pieces.append(jnp.where(low, both[:pairs], both[pairs:]))
            outs[m][f] = jnp.concatenate(pieces, axis=0).astype(jnp.bfloat16)
        return carry

    lax.fori_loop(0, size, one, 0, unroll=True)


def correlate(place, own, halo):
    size, channels, width = own[0].shape
    rows = (GROUP + halo.shape[0] + 1) * channels
    return pl.pallas_call(
        cross_kernel,
        out_shape=[jax.ShapeDtypeStruct((size, channels, 2 * OFFS), jnp.bfloat16)] * GROUP,
        in_specs=[SMEM] + [VMEM] * (GROUP + 1),
        out_specs=[VMEM] * GROUP,
        scratch_shapes=[pltpu.VMEM((size, rows, width), jnp.bfloat16)],
        cost_estimate=pl.CostEstimate(
            flops=2 * size * GROUP * 2 * channels * 128 * width,
            bytes_accessed=2 * size * channels * width * (GROUP + 2),
            transcendentals=0,
        ),
        compiler_params=pltpu.CompilerParams(vmem_limit_bytes=8 << 20),
        name="correlate",
    )(place, *own, halo)


def back(parts, cos_ref, sin_ref, scratch, finish):
    rows = cos_ref.shape[0]
    pitch = odd_pitch(rows)
    base = 0
    for part in parts:
        count, channels, _ = part.shape
        for x in range(count):
            scratch[pl.ds(base + x, channels, stride=pitch), :] = part[x].astype(jnp.float32)
        base += count
    pairs = channels // 2
    for p in range(pairs):
        re = scratch[pl.ds(p * pitch, rows), :].astype(jnp.bfloat16)
        im = scratch[pl.ds((pairs + p) * pitch, rows), :].astype(jnp.bfloat16)
        result = lax.dot_general(re, cos_ref[...], TN, preferred_element_type=jnp.float32)
        result += lax.dot_general(im, sin_ref[...], TN, preferred_element_type=jnp.float32)
        for side in range(2):
            finish(p + side * pairs, result[side * OFFS : (side + 1) * OFFS])


def early_kernel(sets, cos_ref, sin_ref, *refs):
    parts, (out_ref, send_ref, scratch) = refs[:sets], refs[sets:]

    def finish(c, value):
        out_ref[c] = value
        send_ref[c] = value.astype(jnp.bfloat16)

    back(parts, cos_ref, sin_ref, scratch, finish)


def early(cosines, sines, parts):
    rows, lags = cosines.shape
    channels = parts[0].shape[1]
    shape = (channels, OFFS, lags)
    return pl.pallas_call(
        functools.partial(early_kernel, len(parts)),
        out_shape=[
            jax.ShapeDtypeStruct(shape, jnp.float32),
            jax.ShapeDtypeStruct(shape, jnp.bfloat16),
        ],
        in_specs=[VMEM] * (2 + len(parts)),
        out_specs=[VMEM] * 2,
        scratch_shapes=[pltpu.VMEM((channels * odd_pitch(rows), 2 * OFFS), jnp.float32)],
        cost_estimate=pl.CostEstimate(
            flops=4 * rows * channels * OFFS * lags,
            bytes_accessed=6 * channels * OFFS * lags + 4 * rows * channels * OFFS,
            transcendentals=0,
        ),
        compiler_params=pltpu.CompilerParams(vmem_limit_bytes=8 << 20),
        name="early",
    )(cosines, sines, *parts)


def gather_kernel(*refs):
    base = 0
    for part in refs[:-1]:
        refs[-1][base : base + part.shape[0]] = part[...]
        base += part.shape[0]


def gather(parts):
    size, channels, width = parts[0].shape
    return pl.pallas_call(
        gather_kernel,
        out_shape=jax.ShapeDtypeStruct((size * len(parts), channels, width), jnp.bfloat16),
        in_specs=[VMEM] * len(parts),
        out_specs=VMEM,
        compiler_params=pltpu.CompilerParams(vmem_limit_bytes=2 << 20),
        name="gather",
    )(*parts)


def late_kernel(sign_ref, cos_ref, sin_ref, own_ref, other_ref, mine_ref, theirs_ref, *refs):
    out_ref, scratch = refs
    sign = sign_ref[0]

    def finish(c, value):
        out_ref[c] = sign * mine_ref[c] + theirs_ref[c].astype(jnp.float32) + value

    back((own_ref, other_ref), cos_ref, sin_ref, scratch, finish)


def late(sign, cosines, sines, own, other, mine, theirs):
    rows, lags = cosines.shape
    channels = own.shape[1]
    return pl.pallas_call(
        late_kernel,
        out_shape=jax.ShapeDtypeStruct(mine.shape, jnp.float32),
        in_specs=[SMEM] + [VMEM] * 6,
        out_specs=VMEM,
        scratch_shapes=[pltpu.VMEM((channels * odd_pitch(rows), 2 * OFFS), jnp.float32)],
        cost_estimate=pl.CostEstimate(
            flops=4 * rows * channels * OFFS * lags,
            bytes_accessed=10 * channels * OFFS * lags,
            transcendentals=0,
        ),
        compiler_params=pltpu.CompilerParams(vmem_limit_bytes=8 << 20),
        name="late",
    )(sign, cosines, sines, own, other, mine, theirs)


def phases(freq, pos, samples):
    return 2.0 * math.pi / samples * (freq * pos % samples).astype(jnp.float32)


def forward_table(freq, samples):
    times = jnp.arange(samples, dtype=jnp.int32)
    phase = phases(freq[:, :, None], times, samples)
    taper = 0.5 - 0.5 * jnp.cos(2.0 * math.pi / samples * times.astype(jnp.float32))
    both = jnp.stack([taper * jnp.cos(phase), -taper * jnp.sin(phase)], axis=1)
    return both.reshape(-1, samples).astype(jnp.bfloat16)


def inverse_tables(freq, samples, lag_count, factor):
    lagpos = jnp.arange(lag_count, dtype=jnp.int32)[None, :]
    freq = freq[:, None]
    phase = phases(freq, lagpos, samples)
    weight = jnp.where((freq == 0) | (freq == samples // 2), 1.0, 2.0)
    weight = jnp.where(freq > samples // 2, 0.0, weight).astype(jnp.float32) * factor
    return (
        (weight * jnp.cos(phase)).astype(jnp.bfloat16),
        (-weight * jnp.sin(phase)).astype(jnp.bfloat16),
    )


def body(records):
    samples, channels, windows = records.shape
    frequencies = samples // 2 + 1
    halves = lax.axis_size("win")
    blocks = lax.axis_size("cable")
    total_windows = windows * halves
    group = GROUP
    members = group * halves
    halo = -(-OFFS // channels)
    chunks = CHUNKS
    starts = [sum(chunks[:q]) for q in range(len(chunks))]
    assert sum(chunks) * members >= frequencies and blocks % group == 0 and halves == 2
    assert halo < group and channels + OFFS <= 128
    me = lax.axis_index("cable")
    place = lax.rem(me, group)
    half = lax.axis_index("win")

    def exchange(block, m):
        if m == 0:
            return block
        return lax.ppermute(block, "cable", [(i, i ^ m) for i in range(blocks)])

    def sibling(block):
        return lax.ppermute(block, "win", [(i, 1 - i) for i in range(halves)])

    own = jnp.transpose(records, (1, 2, 0))
    other = sibling(own)

    def freqs(q, m, side):
        row = starts[q] + jnp.arange(chunks[q], dtype=jnp.int32)
        return row * members + (place ^ m) * halves + side

    table = jnp.concatenate(
        [
            forward_table(jnp.stack([freqs(q, m, half) for m in range(group)]), samples)
            for q in range(len(chunks))
        ],
        axis=0,
    )
    last = len(chunks) - 1
    lag_count = samples // halves
    factor = 1.0 / math.sqrt(2.0 * total_windows * frequencies)
    sign = jnp.where(half == 0, 1.0, -1.0).astype(jnp.float32)
    freq = jnp.concatenate([freqs(q, m, half) for q in range(last) for m in range(group)])
    early_tables = inverse_tables(freq, samples, lag_count, factor)
    mine, theirs = (
        jnp.concatenate([freqs(last, m, side) for m in range(group)]) for side in (half, 1 - half)
    )
    weights = jnp.concatenate(
        [jnp.full(mine.shape, sign * factor), jnp.full(theirs.shape, factor)]
    )
    late_tables = inverse_tables(
        jnp.concatenate([mine, theirs]), samples, lag_count, weights[:, None]
    )
    table, early_tables, late_tables = lax.optimization_barrier(
        (table, early_tables, late_tables)
    )
    sizes = [size for size in chunks for _ in range(group)]
    white = forward(table, sizes, own, other, total_windows)

    place_arr = place.reshape(1).astype(jnp.int32)
    shares = []
    for q in range(len(chunks)):
        got = {0: white[q * group]}
        for m in ORDER:
            got[m] = exchange(white[q * group + m], m)
        shares.append([got[m] for m in range(group)])
    crosses = []
    for q in range(len(chunks)):
        ahead = edge(place_arr, shares[q], halo, [])
        ahead = lax.ppermute(ahead, "cable", [(i, i - group) for i in range(group, blocks)])
        crosses.append(correlate(place_arr, shares[q], ahead))
    parts = []
    for q in range(len(chunks)):
        got = {0: crosses[q][0]}
        for m in ORDER:
            got[m] = exchange(crosses[q][m], m)
        parts.append([got[m] for m in range(group)])
    mine, send = early(*early_tables, [x for part in parts[:last] for x in part])
    theirs = sibling(send)
    tail = gather(parts[last])
    other_tail = sibling(tail)
    return late(sign.reshape(1), *late_tables, tail, other_tail, mine, theirs)


def solution(mesh):
    return jax.shard_map(
        body,
        mesh=mesh,
        in_specs=(P(None, "cable", "win"),),
        out_specs=P("cable", None, "win"),
        check_vma=False,
    )
```

```python
import functools
import math

import jax
import jax.numpy as jnp
from jax import lax
from jax.experimental import pallas as pl
from jax.experimental.pallas import tpu as pltpu
from jax.sharding import PartitionSpec as P

OFFS = 64
GROUP = 4

epsilon = 1e-06

VMEM = pl.BlockSpec(memory_space=pltpu.VMEM)
SMEM = pl.BlockSpec(memory_space=pltpu.SMEM)
NT = (((1,), (1,)), ((), ()))
TN = (((0,), (0,)), ((), ()))


def odd_pitch(rows):
    return rows + 1 - rows % 2


def forward_kernel(sizes, windows_total, table_ref, own_ref, other_ref, *refs):
    outs, scratch = refs[:-1], refs[-1]
    channels, windows, _ = own_ref.shape
    rows = table_ref.shape[0]
    pitch = odd_pitch(rows)

    def transform(p, carry):
        both = jnp.concatenate(
            [own_ref[2 * p], other_ref[2 * p], own_ref[2 * p + 1], other_ref[2 * p + 1]], axis=0
        )
        spec = lax.dot_general(table_ref[...], both, NT, preferred_element_type=jnp.float32)
        width = 2 * windows
        scratch[pl.ds(2 * p * pitch, rows), :] = spec[:, :width]
        scratch[pl.ds((2 * p + 1) * pitch, rows), :] = spec[:, width:]
        return carry

    for p in range(channels // 2):
        transform(p, 0)

    row = 0
    for size, out in zip(sizes, outs):

        def whiten(f, carry, row=row, size=size, out=out):
            re = scratch[pl.ds(row + f, channels, stride=pitch), :]
            im = scratch[pl.ds(row + size + f, channels, stride=pitch), :]
            power = jnp.sum(re * re + im * im, axis=1, keepdims=True) / windows_total
            scale = lax.rsqrt(power + epsilon)
            out[f, :, : 2 * windows] = (re * scale).astype(jnp.bfloat16)
            out[f, :, 2 * windows :] = (im * scale).astype(jnp.bfloat16)
            return carry

        lax.fori_loop(0, size, whiten, 0, unroll=True)
        row += 2 * size


def forward(table, sizes, own, other, windows_total):
    channels, windows, samples = own.shape
    rows = table.shape[0]
    return pl.pallas_call(
        functools.partial(forward_kernel, sizes, windows_total),
        out_shape=[
            jax.ShapeDtypeStruct((s, channels, 4 * windows), jnp.bfloat16) for s in sizes
        ],
        in_specs=[VMEM] * 3,
        out_specs=[VMEM] * len(sizes),
        scratch_shapes=[pltpu.VMEM((channels * odd_pitch(rows), 2 * windows), jnp.float32)],
        cost_estimate=pl.CostEstimate(
            flops=2 * rows * samples * channels * windows * 2,
            bytes_accessed=4 * channels * windows * samples + 2 * rows * channels * windows * 2,
            transcendentals=0,
        ),
        compiler_params=pltpu.CompilerParams(vmem_limit_bytes=8 << 20),
        name="forward",
    )(table, own, other)


def edge_kernel(place_ref, *refs):
    shares, out_ref = refs[:GROUP], refs[-1]
    for m in range(GROUP):
        block = place_ref[0] ^ m

        @pl.when(block < out_ref.shape[0])
        def _(m=m, block=block):
            out_ref[block] = shares[m][...]


def edge(place, shares, halo):
    shape = (halo,) + shares[0].shape
    return pl.pallas_call(
        edge_kernel,
        out_shape=jax.ShapeDtypeStruct(shape, jnp.bfloat16),
        in_specs=[SMEM] + [VMEM] * GROUP,
        out_specs=VMEM,
        compiler_params=pltpu.CompilerParams(vmem_limit_bytes=4 << 20),
        name="edge",
    )(place, *shares)


def cross_kernel(place_ref, *refs):
    group = GROUP
    own, halo_ref = refs[:group], refs[group]
    outs, rows_ref = refs[group + 1 : -1], refs[-1]
    size, channels, width = own[0].shape
    halo = halo_ref.shape[0]
    half = width // 2
    place = place_ref[0]
    for m in range(group):
        start = pl.multiple_of((place ^ m) * channels, channels)
        rows_ref[:, pl.ds(start, channels), :] = own[m][...]
    for h in range(halo):
        rows_ref[:, pl.ds((group + h) * channels, channels), :] = halo_ref[h]
    breadth = 128
    pairs = channels // 2
    lane = lax.broadcasted_iota(jnp.int32, (pairs, breadth), 1)
    low = lane < OFFS
    reverse = 7 - lax.broadcasted_iota(jnp.int32, (8, breadth), 0)

    def one(f, carry):
        for m in range(group):
            start = pl.multiple_of((place ^ m) * channels, channels)
            left = own[m][f]
            a, b = left[:, :half], left[:, half:]
            lefthand = jnp.concatenate(
                [jnp.concatenate([a, b], axis=1), jnp.concatenate([b, -a], axis=1)], axis=0
            )
            partner = rows_ref[f, pl.ds(start, breadth), :]
            prod = lax.dot_general(lefthand, partner, NT, preferred_element_type=jnp.float32)
            pieces = []
            for part in range(2):
                sides = []
                for side in range(2):
                    first = (2 * part + side) * pairs
                    slabs = []
                    for r in range(0, pairs, 8):
                        slab = jnp.take_along_axis(
                            prod[first + r : first + r + 8], reverse, axis=0
                        )
                        shift = (breadth - 8 - side * (pairs - OFFS) - r) % breadth
                        slabs.append(pltpu.roll(slab, shift, 1, stride=1, stride_axis=0))
                    sides.append(jnp.concatenate(slabs, axis=0))
                pieces.append(jnp.where(low, *sides))
            outs[m][f] = jnp.concatenate(pieces, axis=0).astype(jnp.bfloat16)
        return carry

    lax.fori_loop(0, size, one, 0, unroll=True)


def correlate(place, own, halo):
    size, channels, width = own[0].shape
    rows = (GROUP + halo.shape[0] + 1) * channels
    return pl.pallas_call(
        cross_kernel,
        out_shape=[jax.ShapeDtypeStruct((size, channels, 2 * OFFS), jnp.bfloat16)] * GROUP,
        in_specs=[SMEM] + [VMEM] * (GROUP + 1),
        out_specs=[VMEM] * GROUP,
        scratch_shapes=[pltpu.VMEM((size, rows, width), jnp.bfloat16)],
        cost_estimate=pl.CostEstimate(
            flops=2 * size * GROUP * 2 * channels * 128 * width,
            bytes_accessed=2 * size * channels * width * (GROUP + 2),
            transcendentals=0,
        ),
        compiler_params=pltpu.CompilerParams(vmem_limit_bytes=8 << 20),
        name="correlate",
    )(place, *own, halo)


def back(parts, cos_ref, sin_ref, scratch, finish):
    rows = cos_ref.shape[0]
    pitch = odd_pitch(rows)
    base = 0
    for part in parts:
        count, channels, _ = part.shape
        for x in range(count):
            scratch[pl.ds(base + x, channels, stride=pitch), :] = part[x].astype(jnp.float32)
        base += count
    pairs = channels // 2
    for p in range(pairs):
        re = scratch[pl.ds(p * pitch, rows), :].astype(jnp.bfloat16)
        im = scratch[pl.ds((pairs + p) * pitch, rows), :].astype(jnp.bfloat16)
        result = lax.dot_general(re, cos_ref[...], TN, preferred_element_type=jnp.float32)
        result += lax.dot_general(im, sin_ref[...], TN, preferred_element_type=jnp.float32)
        channel = p // 8 * 8 + 7 - p % 8
        for side in range(2):
            finish(channel + side * pairs, result[side * OFFS : (side + 1) * OFFS])


def early_kernel(sets, cos_ref, sin_ref, *refs):
    parts, (out_ref, send_ref, scratch) = refs[:sets], refs[sets:]

    def finish(c, value):
        out_ref[c] = value
        send_ref[c] = value.astype(jnp.bfloat16)

    back(parts, cos_ref, sin_ref, scratch, finish)


def early(cosines, sines, parts):
    rows, lags = cosines.shape
    channels = parts[0].shape[1]
    shape = (channels, OFFS, lags)
    return pl.pallas_call(
        functools.partial(early_kernel, len(parts)),
        out_shape=[
            jax.ShapeDtypeStruct(shape, jnp.float32),
            jax.ShapeDtypeStruct(shape, jnp.bfloat16),
        ],
        in_specs=[VMEM] * (2 + len(parts)),
        out_specs=[VMEM] * 2,
        scratch_shapes=[pltpu.VMEM((channels * odd_pitch(rows), 2 * OFFS), jnp.float32)],
        cost_estimate=pl.CostEstimate(
            flops=4 * rows * channels * OFFS * lags,
            bytes_accessed=6 * channels * OFFS * lags + 4 * rows * channels * OFFS,
            transcendentals=0,
        ),
        compiler_params=pltpu.CompilerParams(vmem_limit_bytes=8 << 20),
        name="early",
    )(cosines, sines, *parts)


def gather_kernel(*refs):
    base = 0
    for part in refs[:-1]:
        refs[-1][base : base + part.shape[0]] = part[...]
        base += part.shape[0]


def gather(parts):
    size, channels, width = parts[0].shape
    return pl.pallas_call(
        gather_kernel,
        out_shape=jax.ShapeDtypeStruct((size * len(parts), channels, width), jnp.bfloat16),
        in_specs=[VMEM] * len(parts),
        out_specs=VMEM,
        compiler_params=pltpu.CompilerParams(vmem_limit_bytes=2 << 20),
        name="gather",
    )(*parts)


def late_kernel(
    sign_ref, cos_ref, sin_ref, own_ref, other_ref, mine_ref, theirs_ref, out_ref, *scratches
):
    scratch, lags_ref, sems = scratches
    sign = sign_ref[0]
    pairs = own_ref.shape[1] // 2
    count = sems.shape[0] // 2
    span = pairs // count
    copies = []

    def finish(c, value):
        lags_ref[c] = sign * mine_ref[c] + theirs_ref[c].astype(jnp.float32) + value
        if c % span == 0:
            copy = pltpu.make_async_copy(
                lags_ref.at[pl.ds(c, span)],
                out_ref.at[pl.ds(c, span)],
                sems.at[c // span],
            )
            copy.start()
            copies.append(copy)

    back((own_ref, other_ref), cos_ref, sin_ref, scratch, finish)
    for copy in copies:
        copy.wait()


def late(sign, cosines, sines, own, other, mine, theirs):
    rows, lags = cosines.shape
    channels = own.shape[1]
    return pl.pallas_call(
        late_kernel,
        out_shape=jax.ShapeDtypeStruct(mine.shape, jnp.float32),
        in_specs=[SMEM] + [VMEM] * 6,
        out_specs=pl.BlockSpec(memory_space=pl.ANY),
        scratch_shapes=[
            pltpu.VMEM((channels * odd_pitch(rows), 2 * OFFS), jnp.float32),
            pltpu.VMEM(mine.shape, jnp.float32),
            pltpu.SemaphoreType.DMA((8,)),
        ],
        cost_estimate=pl.CostEstimate(
            flops=4 * rows * channels * OFFS * lags,
            bytes_accessed=10 * channels * OFFS * lags,
            transcendentals=0,
        ),
        compiler_params=pltpu.CompilerParams(vmem_limit_bytes=8 << 20),
        name="late",
    )(sign, cosines, sines, own, other, mine, theirs)


def phases(freq, pos, samples):
    return 2.0 * math.pi / samples * (freq * pos % samples).astype(jnp.float32)


def forward_table(freq, samples):
    times = jnp.arange(samples, dtype=jnp.int32)
    phase = phases(freq[:, :, None], times, samples)
    taper = 0.5 - 0.5 * jnp.cos(2.0 * math.pi / samples * times.astype(jnp.float32))
    both = jnp.stack([taper * jnp.cos(phase), -taper * jnp.sin(phase)], axis=1)
    return both.reshape(-1, samples).astype(jnp.bfloat16)


def inverse_tables(freq, samples, lag_count, factor):
    lagpos = jnp.arange(lag_count, dtype=jnp.int32)[None, :]
    freq = freq[:, None]
    phase = phases(freq, lagpos, samples)
    weight = jnp.where((freq == 0) | (freq == samples // 2), 1.0, 2.0)
    weight = jnp.where(freq > samples // 2, 0.0, weight).astype(jnp.float32) * factor
    return (
        (weight * jnp.cos(phase)).astype(jnp.bfloat16),
        (-weight * jnp.sin(phase)).astype(jnp.bfloat16),
    )


def body(records):
    samples, channels, windows = records.shape
    frequencies = samples // 2 + 1
    halves = lax.axis_size("win")
    blocks = lax.axis_size("cable")
    total_windows = windows * halves
    group = GROUP
    members = group * halves
    halo = -(-OFFS // channels)
    slots = -(-frequencies // members)
    most = -(-4 * slots // 11)
    chunks = (most, most, slots - 2 * most)
    starts = [sum(chunks[:q]) for q in range(len(chunks))]
    assert blocks % group == 0 and halves == 2
    assert halo < group and channels + OFFS <= 128
    me = lax.axis_index("cable")
    place = lax.rem(me, group)
    half = lax.axis_index("win")

    def exchange(block, m):
        if m == 0:
            return block
        return lax.ppermute(block, "cable", [(i, i ^ m) for i in range(blocks)])

    def sibling(block):
        return lax.ppermute(block, "win", [(i, 1 - i) for i in range(halves)])

    own = jnp.transpose(records, (1, 2, 0))
    other = sibling(own)

    def freqs(q, m, side):
        row = starts[q] + jnp.arange(chunks[q], dtype=jnp.int32)
        return row * members + (place ^ m) * halves + side

    table = jnp.concatenate(
        [
            forward_table(jnp.stack([freqs(q, m, half) for m in range(group)]), samples)
            for q in range(len(chunks))
        ],
        axis=0,
    )
    last = len(chunks) - 1
    lag_count = samples // halves
    factor = 1.0 / math.sqrt(2.0 * total_windows * frequencies)
    sign = jnp.where(half == 0, 1.0, -1.0).astype(jnp.float32)
    freq = jnp.concatenate([freqs(q, m, half) for q in range(last) for m in range(group)])
    early_tables = inverse_tables(freq, samples, lag_count, factor)
    mine, theirs = (
        jnp.concatenate([freqs(last, m, side) for m in range(group)]) for side in (half, 1 - half)
    )
    weights = jnp.concatenate(
        [jnp.full(mine.shape, sign * factor), jnp.full(theirs.shape, factor)]
    )
    late_tables = inverse_tables(
        jnp.concatenate([mine, theirs]), samples, lag_count, weights[:, None]
    )
    table, early_tables, late_tables = lax.optimization_barrier(
        (table, early_tables, late_tables)
    )
    sizes = [size for size in chunks for _ in range(group)]
    white = forward(table, sizes, own, other, total_windows)

    place_arr = place.reshape(1).astype(jnp.int32)
    shares = []
    for q in range(len(chunks)):
        got = {0: white[q * group]}
        for m in range(1, group):
            got[m] = exchange(white[q * group + m], m)
        shares.append([got[m] for m in range(group)])
    crosses = []
    for q in range(len(chunks)):
        ahead = edge(place_arr, shares[q], halo)
        ahead = lax.ppermute(ahead, "cable", [(i, i - group) for i in range(group, blocks)])
        crosses.append(correlate(place_arr, shares[q], ahead))
    parts = []
    for q in range(len(chunks)):
        got = {0: crosses[q][0]}
        for m in range(1, group):
            got[m] = exchange(crosses[q][m], m)
        parts.append([got[m] for m in range(group)])
    mine, send = early(*early_tables, [x for part in parts[:last] for x in part])
    theirs = sibling(send)
    tail = gather(parts[last])
    other_tail = sibling(tail)
    return late(sign.reshape(1), *late_tables, tail, other_tail, mine, theirs)


def solution(mesh):
    return jax.shard_map(
        body,
        mesh=mesh,
        in_specs=(P(None, "cable", "win"),),
        out_specs=P("cable", None, "win"),
        check_vma=False,
    )
```
